32 devices in a mesh: seq: 8 (over z, core), head: 4 (over y, x).
Axes of the slice: x: 2, y: 2, z: 4, core: 2. Of those that a mesh axis runs over, the one named last changes fastest.
Arguments:
- qk_proj: bfloat16 [1024, 128], P('seq'), may hold values from -0.5 to 0.5
- values: bfloat16 [1024, 5120], P('seq', 'head'), may hold values from -0.59765625 to 0.59765625
- out_grad: bfloat16 [1024, 5120], P('seq', 'head'), may hold values from -1.5 to 1.5
- level_weights: float32 [80, 16, 1024], P('head', None, 'seq'), may hold values from 0.05 to 1
Outputs:
- qk_grad: float32 [1024, 128], P(('seq', 'head'))
- value_grad: bfloat16 [1024, 5120], P('seq', 'head')
- level_grad: float32 [80, 16, 1024], P('head', None, 'seq')
- carried_state: float32 [8, 128, 5120], P('seq', None, 'head')
The draws below stay inside these ranges and needn't reach their ends.
All inputs are finite; a program needn't handle non-finite values.
Results may differ from the reference program's by a relative error of at most 0.0057.
Values sent between devices are 32-bit elements; how exact they have to be, the bound alone decides.
A program may use at most 64 MiB of HBM per device.

```python
import math
import jax
import jax.numpy as jnp
from jax import lax

HEADS = 80
HEAD_DIM = 64
STATE_DIM = 128
LEVELS = 16
TOK_DEV = 128
TOKENS = 1024
TOK_BITS = 7
SEQ_BITS = 3


def steps_of(key, extent, split, low, high):
    loudness, own = 1.0, jax.random.fold_in(key, 6)
    for axis_at, parts in split:
        draws = jnp.exp(jax.random.uniform(jax.random.fold_in(own, axis_at), (parts,), jnp.float32, low / len(split), high / len(split)))
        loudness = loudness * jnp.repeat(draws, extent[axis_at] // parts).reshape([-1 if axis == axis_at else 1 for axis in range(len(extent))])
    return loudness


def noise(stream_key, extent, scale, most, cuts=(), kind=jnp.bfloat16):
    result = scale * jax.random.normal(stream_key, extent, jnp.float32)
    if cuts:
        result = result * steps_of(stream_key, extent, cuts, -0.22, 0.18)
    return jnp.clip(result, -most, most).astype(kind)


def setup_inputs(seed: int = 0) -> dict:
    splits = jax.random.split(jax.random.key(seed), 5)
    return {
        "qk_proj": noise(splits[0], (TOKENS, STATE_DIM), STATE_DIM ** -0.5, 0.5, ((0, 8),)),
        "values": noise(splits[1], (TOKENS, HEADS * HEAD_DIM), 0.1, 0.59765625, ((0, 8), (1, 4))),
        "out_grad": noise(splits[2], (TOKENS, HEADS * HEAD_DIM), 0.25, 1.5, ((0, 8), (1, 4))),
        "level_weights": jnp.clip(jnp.exp(math.log(1.0) - 2.9957323 * jax.random.uniform(splits[3], (HEADS, LEVELS, TOKENS), jnp.float32) ** steps_of(splits[3], (HEADS, LEVELS, TOKENS), ((0, 4), (2, 8)), -0.2, 0.2)), 0.05, 1.0),
    }


def level_table(length, tok_bits):
    positions = jnp.arange(length, dtype=jnp.int32)
    crossed = jnp.bitwise_xor(positions[:, None], positions[None, :])
    level_map = jnp.zeros((length, length), jnp.int32)
    for exponent in range(tok_bits):
        level_map = level_map + (crossed >= (1 << exponent)).astype(jnp.int32)
    return jnp.where(positions[None, :] <= positions[:, None], level_map, -1)


def scale_grads(grads_seg, weights_seg):
    cross_weights = weights_seg[:, TOK_BITS + 1:TOK_BITS + 1 + SEQ_BITS, :]
    column_scale = jnp.repeat(jnp.transpose(cross_weights, (1, 2, 0)), HEAD_DIM, axis=2)
    return (column_scale * grads_seg.astype(jnp.float32)[None]).astype(jnp.bfloat16)


def reference(qk_proj, values, out_grad, level_weights):
    segments = TOKENS // TOK_DEV
    inner_width = HEADS * HEAD_DIM
    keys_all = qk_proj.reshape(segments, TOK_DEV, STATE_DIM)
    vals_all = values.reshape(segments, TOK_DEV, inner_width)
    grads_all = out_grad.reshape(segments, TOK_DEV, inner_width)
    weights_all = jnp.transpose(level_weights.reshape(HEADS, LEVELS, segments, TOK_DEV), (2, 0, 1, 3))

    block_state = lax.map(lambda operands: jnp.dot(operands[0].T, operands[1], preferred_element_type=jnp.float32), (keys_all, vals_all))
    grad_state = lax.map(lambda operands: jnp.einsum("tn,btx->bnx", operands[0].astype(jnp.float32), scale_grads(operands[1], operands[2]).astype(jnp.float32)), (keys_all, grads_all, weights_all))

    indices = jnp.arange(segments, dtype=jnp.int32)
    forward_rows = []
    backward_rows = []
    for bit_pos in range(SEQ_BITS):
        shifted = jnp.right_shift(indices, bit_pos)
        high_bit = jnp.bitwise_and(shifted, 1)
        forward_rows.append(((shifted[None, :] == shifted[:, None] - 1) & (high_bit[:, None] == 1)).astype(jnp.float32))
        backward_rows.append(((shifted[None, :] == shifted[:, None] + 1) & (high_bit[:, None] == 0)).astype(jnp.float32))
    forward_pick = jnp.stack(forward_rows, axis=1)
    backward_pick = jnp.stack(backward_rows, axis=1)
    level_map = level_table(TOK_DEV, TOK_BITS)

    def one_segment(operands):
        keys_seg, vals_seg, grads_seg, weights_seg, pick_forward, pick_backward = operands
        level_state = jnp.einsum("bf,fnx->bnx", pick_forward, block_state, precision=lax.Precision.HIGHEST)
        back_state = jnp.einsum("bf,fbnx->nx", pick_backward, grad_state, precision=lax.Precision.HIGHEST)
        carried = jnp.sum(level_state, axis=0)
        state_low = level_state.astype(jnp.bfloat16)
        back_low = back_state.astype(jnp.bfloat16)
        scaled = scale_grads(grads_seg, weights_seg)
        grad_float = grads_seg.astype(jnp.float32)
        query_cross = jnp.einsum("btx,bnx->tn", scaled.astype(jnp.float32), state_low.astype(jnp.float32))
        key_cross = jnp.dot(vals_seg, back_low.T, preferred_element_type=jnp.float32)
        value_cross = jnp.dot(keys_seg, back_low, preferred_element_type=jnp.float32)
        readout = jnp.einsum("tn,bnx->btx", keys_seg.astype(jnp.float32), state_low.astype(jnp.float32))
        lam_cross = jnp.sum((readout * grad_float[None]).reshape(SEQ_BITS, TOK_DEV, HEADS, HEAD_DIM), axis=3)
        lam_cross = jnp.transpose(lam_cross, (2, 0, 1))

        score = jnp.dot(keys_seg, keys_seg.T, preferred_element_type=jnp.float32)
        keys_float = keys_seg.astype(jnp.float32)
        vals_heads = jnp.transpose(vals_seg.reshape(TOK_DEV, HEADS, HEAD_DIM).astype(jnp.float32), (1, 0, 2))
        grads_heads = jnp.transpose(grads_seg.reshape(TOK_DEV, HEADS, HEAD_DIM).astype(jnp.float32), (1, 0, 2))
        local_levels = weights_seg[:, :TOK_BITS + 1, :]

        def one_head(head_ops):
            weights_head, grads_head, vals_head = head_ops
            pair_grad = jnp.einsum("tp,sp->ts", grads_head, vals_head)
            local_weight = jnp.zeros((TOK_DEV, TOK_DEV), jnp.float32)
            for level_number in range(TOK_BITS + 1):
                local_weight = local_weight + jnp.where(level_map == level_number, weights_head[level_number, :, None], 0.0)
            weighted_score = (local_weight * score).astype(jnp.bfloat16).astype(jnp.float32)
            weighted_grad = (local_weight * pair_grad).astype(jnp.bfloat16).astype(jnp.float32)
            value_head = jnp.einsum("ts,tp->sp", weighted_score, grads_head)
            qk_head = jnp.einsum("ts,sn->tn", weighted_grad, keys_float) + jnp.einsum("ts,tn->sn", weighted_grad, keys_float)
            product = score * pair_grad
            lam_head = jnp.stack([jnp.sum(jnp.where(level_map == level_number, product, 0.0), axis=1) for level_number in range(TOK_BITS + 1)], axis=0)
            return value_head, qk_head, lam_head

        value_heads, qk_heads, lam_local = lax.map(one_head, (local_levels, grads_heads, vals_heads))
        value_local = jnp.transpose(value_heads, (1, 0, 2)).reshape(TOK_DEV, inner_width)
        qk_local = jnp.sum(qk_heads, axis=0)
        unused_levels = LEVELS - TOK_BITS - 1 - SEQ_BITS
        lam_all = jnp.concatenate([lam_local, lam_cross, jnp.zeros((HEADS, unused_levels, TOK_DEV), jnp.float32)], axis=1)
        value_grad_seg = (value_local + value_cross).astype(jnp.bfloat16)
        qk_seg = qk_local + query_cross + key_cross
        return qk_seg, value_grad_seg, lam_all, carried

    qk_parts, value_parts, lam_parts, carried_parts = lax.map(one_segment, (keys_all, vals_all, grads_all, weights_all, forward_pick, backward_pick))
    qk_grad = qk_parts.reshape(TOKENS, STATE_DIM)
    value_grad = value_parts.reshape(TOKENS, inner_width)
    level_grad = jnp.transpose(lam_parts, (1, 2, 0, 3)).reshape(HEADS, LEVELS, TOKENS)
    return qk_grad, value_grad, level_grad, carried_parts
```

```python
import functools

import jax
import jax.numpy as jnp
from jax import lax
from jax.experimental import pallas as pl
from jax.experimental.pallas import tpu as pltpu
from jax.sharding import PartitionSpec as P

MESH = pl.DeviceIdType.MESH
CHUNKS = 4
F32 = jnp.float32
BF16 = jnp.bfloat16


def dot(a, b, ca, cb):
    return lax.dot_general(a, b, (((ca,), (cb,)), ((), ())), preferred_element_type=F32)


class Ids:
    def __init__(self):
        self.table = {}

    def __call__(self, *key):
        return self.table.setdefault(key, len(self.table))


def sem_ids(chips, heads, chip_bits):
    send, recv = Ids(), Ids()
    for r in range(CHUNKS):
        for ids in (send, recv):
            ids("xa", r), ids("xb", r), ids("rd", r)
            for k in range(chip_bits):
                ids("xd", k, r), ids("ru", k, r)
                ids("up", k, r), ids("dn", k, r)
        for k in range(chip_bits):
            send("dc", k, r)
            for i in range(1 << k):
                send("up", k, r, i), send("dn", k, r, i)
                recv("dc", k, r, i)
    send("xc"), recv("xc")
    for i in range(heads):
        send("rs", i), recv("rs", i)
    return send, recv


def kernel(chips, head_parts, seq_bits, qk_ref, v_ref, g_ref, lw_ref, qg_ref, vg_ref, lam_ref, car_ref,
           own, gst, xup, xd0, xd, bz, gz, acc, dsum, lst, dcon, drec, bh, bo, bst, low, blow, sc, vloc, at, qp, rs,
           lev_ref, ssem, rsem):
    tok, state = qk_ref.shape
    width = v_ref.shape[1]
    nheads, levels = lw_ref.shape[0], lw_ref.shape[1]
    hdim = width // nheads
    tok_bits = tok.bit_length() - 1
    chip_bits = seq_bits - 1
    half = state // 2
    rows = half // CHUNKS
    sid, rid = sem_ids(chips, head_parts, chip_bits)

    seq, hd = lax.axis_index("seq"), lax.axis_index("head")
    core, z = seq % 2, seq // 2
    partner = seq + 1 - 2 * core

    def bit(k):
        return (z // (1 << k)) % 2

    def at_chip(chip):
        return {"seq": chip * 2 + core}

    mines = [pl.ds(pl.multiple_of(core * half + r * rows, rows), rows) for r in range(CHUNKS)]
    others = [pl.ds(pl.multiple_of((1 - core) * half + r * rows, rows), rows) for r in range(CHUNKS)]
    mine, other = mines.__getitem__, others.__getitem__

    def part(r):
        return pl.ds(r * rows, rows)

    started = []

    def send(cond, src, dst, skey, rkey, device):
        pltpu.make_async_remote_copy(
            src_ref=src, dst_ref=dst, send_sem=ssem.at[sid(*skey)], recv_sem=rsem.at[rid(*rkey)],
            device_id=device, device_id_type=MESH).start()
        started.append((cond, skey))

    def sent(skey):
        like = xd0 if skey[0] == "xc" else rs.at[skey[1]] if skey[0] == "rs" else bz.at[part(0)]
        pltpu.make_async_remote_copy(
            src_ref=like, dst_ref=like, send_sem=ssem.at[sid(*skey)], recv_sem=rsem.at[0],
            device_id={"seq": partner}, device_id_type=MESH).wait_send()

    def arrive(ref, rkey):
        pltpu.make_async_remote_copy(
            src_ref=ref, dst_ref=ref, send_sem=ssem.at[0], recv_sem=rsem.at[rid(*rkey)],
            device_id={"seq": partner}, device_id_type=MESH).wait_recv()

    barrier = pltpu.get_barrier_semaphore()
    pl.semaphore_signal(barrier, inc=1, device_id={"seq": partner}, device_id_type=MESH)
    for i in range(1, chips):
        pl.semaphore_signal(barrier, inc=1, device_id=at_chip((z + i) % chips), device_id_type=MESH)
    for i in range(1, head_parts):
        pl.semaphore_signal(barrier, inc=1, device_id={"head": (hd + i) % head_parts}, device_id_type=MESH)

    qk = qk_ref[...]
    own[...] = dot(qk, v_ref[...], 0, 0)
    pl.semaphore_wait(barrier, 1 + (chips - 1) + (head_parts - 1))
    for r in range(CHUNKS):
        send(None, own.at[other(r)], xup.at[other(r)], ("xa", r), ("xa", r), {"seq": partner})

    spread = (lax.broadcasted_iota(jnp.int32, (nheads, width), 1) // hdim
              == lax.broadcasted_iota(jnp.int32, (nheads, width), 0)).astype(F32).astype(BF16)

    def grad_state(b):
        weight = lw_ref[:, tok_bits + 1 + b, :]
        first = weight.astype(BF16)
        rest = weight - first.astype(F32)
        second = rest.astype(BF16)
        third = (rest - second.astype(F32)).astype(BF16)
        scale = dot(first, spread, 0, 0) + (dot(second, spread, 0, 0) + dot(third, spread, 0, 0))
        scaled = (scale * g_ref[...].astype(F32)).astype(BF16)
        sc[b] = scaled
        gst[b] = dot(qk, scaled, 0, 0)

    for k in range(chip_bits - 1, -1, -1):
        grad_state(k + 1)
        for r in range(CHUNKS):
            send(None, gst.at[k + 1, other(r)], xd.at[k, part(r)], ("xd", k, r), ("xd", k, r), {"seq": partner})

    for r in range(CHUNKS):
        arrive(xup.at[mine(r)], ("xa", r))
        bz[part(r)] = own[mine(r)] + xup[mine(r)]
        if chip_bits:
            cond = bit(0) == 0

            @pl.when(cond)
            def _():
                send(cond, bz.at[part(r)], lst.at[0, mine(r)], ("up", 0, r, 0), ("up", 0, r), at_chip(z + 1))

        for k in range(chip_bits - 1, -1, -1):
            arrive(xd.at[k, part(r)], ("xd", k, r))
            gz[k, part(r)] = gst[k + 1, mine(r)] + xd[k, part(r)]
            size = 1 << k
            under = z % size
            if k == 0:
                cond_d = bit(0) == 1

                @pl.when(cond_d)
                def _():
                    send(cond_d, gz.at[0, part(r)], drec.at[0, part(r)], ("dn", 0, r, 0), ("dn", 0, r), at_chip(z - 1))
            for i in range(1, size):
                cond_c = (bit(k) == 1) & (under == i)

                @pl.when(cond_c)
                def _():
                    send(cond_c, gz.at[k, part(r)], dcon.at[size - 1 - k + i - 1, part(r)],
                         ("dc", k, r), ("dc", k, r, i), at_chip(z - i))

    cond_low = core == 0
    cond_high = core == 1

    @pl.when(cond_low)
    def _():
        for r in range(CHUNKS):
            send(cond_low, own.at[mine(r)], xup.at[mine(r)], ("xb", r), ("xb", r), {"seq": partner})

    grad_state(0)

    @pl.when(cond_high)
    def _():
        send(cond_high, gst.at[0], xd0, ("xc",), ("xc",), {"seq": partner})

    key_at = lax.broadcasted_iota(jnp.int32, (tok, tok), 0)
    query_at = lax.broadcasted_iota(jnp.int32, (tok, tok), 1)
    crossed = key_at ^ query_at
    found = jnp.zeros((tok, tok), jnp.int32)
    for exponent in range(tok_bits):
        found = found + jnp.where(crossed >= (1 << exponent), 1, 0)
    lev_ref[0] = jnp.where(key_at <= query_at, found, -1).astype(F32)
    lev_ref[1] = dot(qk, qk, 1, 1)
    at[...] = jnp.zeros_like(at)
    lam_ref[:, tok_bits + 1 + seq_bits:, :] = jnp.zeros((nheads, levels - tok_bits - 1 - seq_bits, tok), F32)

    def head_group(head, cols, count):
        vals, grads = v_ref[:, cols], g_ref[:, cols]
        lane_head = lax.broadcasted_iota(jnp.int32, vals.shape, 1) // hdim
        score_parts, grad_parts = [], []
        total = at[...]
        for j in range(count):
            vals_j = vals if count == 1 else jnp.where(lane_head == j, vals, jnp.zeros_like(vals))
            grads_j = grads if count == 1 else jnp.where(lane_head == j, grads, jnp.zeros_like(grads))
            pair = dot(vals_j, grads, 1, 1)
            lev, score = lev_ref[0], lev_ref[1]
            weights = lw_ref[head + j]
            product = score * pair
            local = jnp.zeros((tok, tok), F32)
            sums = []
            for level in range(tok_bits + 1):
                here = lev == float(level)
                local = jnp.where(here, weights[level:level + 1, :], local)
                sums.append(jnp.sum(jnp.where(here, product, 0.0), axis=0, keepdims=True))
            lam_ref[head + j, 0:tok_bits + 1, :] = jnp.concatenate(sums, axis=0)
            score_parts.append((local * score).astype(BF16))
            grad_parts.append(grads_j)
            total = total + (local * pair).astype(BF16).astype(F32)
        at[...] = total
        out = dot(score_parts[0], grad_parts[0], 1, 0)
        for j in range(1, count):
            out = out + dot(score_parts[j], grad_parts[j], 1, 0)
        vloc[:, cols] = out

    per = max(1, 128 // hdim)
    groups = nheads // per

    def run_groups(start, stop):
        @pl.loop(start, stop)
        def _(p):
            head_group(p * per, pl.ds(pl.multiple_of(p * per * hdim, per * hdim), per * hdim), per)

    def up_step(k, r):
        cond = bit(k) == 1

        @pl.when(cond)
        def _():
            arrive(lst.at[k, mine(r)], ("up", k, r))
            send(cond, lst.at[k, mine(r)], lst.at[k, mine(r)], ("ru", k, r), ("ru", k, r), {"seq": partner})

        kk = k + 1
        if kk < chip_bits:
            size = 1 << kk
            cond_s = (z % size == size - 1) & (bit(kk) == 0)

            @pl.when(cond_s)
            def _():
                value = bz[part(r)]
                for j in range(kk):
                    value = value + lst[j, mine(r)]
                acc[kk, part(r)] = value
                for i in range(size - 1, -1, -1):
                    send(cond_s, acc.at[kk, part(r)], lst.at[kk, mine(r)], ("up", kk, r, i), ("up", kk, r),
                         at_chip(z + 1 + i))

            cond_d = (z % size == 0) & (bit(kk) == 1)

            @pl.when(cond_d)
            def _():
                value = gz[kk, part(r)]
                for i in range(1, size):
                    slot = size - 1 - kk + i - 1
                    arrive(dcon.at[slot, part(r)], ("dc", kk, r, i))
                    value = value + dcon[slot, part(r)]
                dsum[kk, part(r)] = value
                for i in range(size):
                    send(cond_d, dsum.at[kk, part(r)], drec.at[kk, part(r)], ("dn", kk, r, i), ("dn", kk, r),
                         at_chip(z - size + i))

    has_back = z != chips - 1

    def down_step(r):
        bh[part(r)] = jnp.zeros((rows, width), F32)
        for k in range(chip_bits):
            @pl.when(bit(k) == 0)
            def _():
                arrive(drec.at[k, part(r)], ("dn", k, r))
                bh[part(r)] = bh[part(r)] + drec[k, part(r)]

        @pl.when(has_back)
        def _():
            send(has_back, bh.at[part(r)], bo.at[part(r)], ("rd", r), ("rd", r), {"seq": partner})

    def cross(b):
        state_low = low[b]
        readout = dot(qk, state_low, 1, 0)
        product = readout * g_ref[...].astype(F32)
        high = product.astype(BF16)
        rest = (product - high.astype(F32)).astype(BF16)
        lam_ref[:, tok_bits + 1 + b, :] = dot(spread, high, 1, 1) + dot(spread, rest, 1, 1)
        part_b = dot(sc[b], state_low, 1, 1)
        if b == 0:
            qp[...] = part_b
        else:
            qp[...] = qp[...] + part_b

    def level_zero():
        @pl.when(core == 1)
        def _():
            for r in range(CHUNKS):
                arrive(xup.at[other(r)], ("xb", r))
            low[0] = xup[...].astype(BF16)
            car_ref[0] = xup[...]

        @pl.when(core == 0)
        def _():
            low[0] = jnp.zeros((state, width), BF16)
            car_ref[0] = jnp.zeros((state, width), F32)

        cross(0)

    def level_up(k):
        cond = bit(k) == 1

        @pl.when(cond)
        def _():
            for r in range(CHUNKS):
                arrive(lst.at[k, other(r)], ("ru", k, r))
            low[k + 1] = lst[k].astype(BF16)
            car_ref[0] = car_ref[0] + lst[k]

        @pl.when(jnp.logical_not(cond))
        def _():
            low[k + 1] = jnp.zeros((state, width), BF16)

        cross(k + 1)

    steps = [(lambda r=r: up_step(0, r)) for r in range(CHUNKS)] if chip_bits else []
    steps.append(level_zero)
    for k in range(1, chip_bits):
        if k == chip_bits - 1:
            for r in range(CHUNKS):
                steps.append(lambda r=r, k=k: (up_step(k, r), down_step(r)))
        else:
            steps += [(lambda r=r, k=k: up_step(k, r)) for r in range(CHUNKS)]
    if chip_bits < 2:
        steps += [(lambda r=r: down_step(r)) for r in range(CHUNKS)]
    slots = min(5, max(1, groups))
    done = 0
    for n, step in enumerate(steps):
        upto = groups * min(slots, n * slots // len(steps) + 1) // slots
        if upto > done:
            run_groups(done, upto)
            done = upto
        step()
    if done < groups:
        run_groups(done, groups)
    for h in range(groups * per, nheads):
        head_group(h, pl.ds(h * hdim, hdim), 1)

    high = at[...].astype(BF16)
    rest = (at[...] - high.astype(F32)).astype(BF16)
    qp[...] = qp[...] + (dot(high, qk, 1, 0) + dot(high, qk, 0, 0)) + (dot(rest, qk, 1, 0) + dot(rest, qk, 0, 0))

    for k in range(chip_bits):
        level_up(k)

    @pl.when(has_back)
    def _():
        for r in range(CHUNKS):
            arrive(bo.at[part(r)], ("rd", r))
            bst[mine(r)] = bh[part(r)]
            bst[other(r)] = bo[part(r)]

    @pl.when(jnp.logical_not(has_back))
    def _():
        bst[...] = jnp.zeros((state, width), F32)

    @pl.when(core == 0)
    def _():
        arrive(xd0, ("xc",))
        blow[...] = (bst[...] + xd0[...]).astype(BF16)

    @pl.when(core == 1)
    def _():
        blow[...] = bst[...].astype(BF16)

    back = blow[...]
    qp[...] = qp[...] + dot(v_ref[...], back, 1, 1)
    share = tok // head_parts
    for i in range(1, head_parts):
        to = (hd + i) % head_parts
        send(None, qp.at[pl.ds(pl.multiple_of(to * share, share), share)], rs.at[i], ("rs", i), ("rs", i), {"head": to})
    vg_ref[...] = (vloc[...] + dot(qk, back, 1, 0)).astype(BF16)
    total = qp[pl.ds(pl.multiple_of(hd * share, share), share)]
    for i in range(1, head_parts):
        arrive(rs.at[i], ("rs", i))
        total = total + rs[i]
    qg_ref[...] = total

    for cond, skey in started:
        if cond is None:
            sent(skey)
        else:
            @pl.when(cond)
            def _():
                sent(skey)


def solution(mesh):
    chips = mesh.shape["seq"] // 2
    head_parts = mesh.shape["head"]
    seq_bits = mesh.shape["seq"].bit_length() - 1
    chip_bits = seq_bits - 1

    def body(qk_proj, values, out_grad, level_weights):
        tok, state = qk_proj.shape
        width = values.shape[1]
        nheads, levels = level_weights.shape[:2]
        half = state // 2
        send, recv = sem_ids(chips, head_parts, chip_bits)
        bits = max(1, chip_bits)
        slots = max(1, (1 << chip_bits) - 1 - chip_bits)
        vm = pltpu.VMEM
        vspec = pl.BlockSpec(memory_space=pltpu.VMEM)
        return pl.pallas_call(
            functools.partial(kernel, chips, head_parts, seq_bits),
            out_shape=(
                jax.ShapeDtypeStruct((tok // head_parts, state), F32),
                jax.ShapeDtypeStruct((tok, width), BF16),
                jax.ShapeDtypeStruct((nheads, levels, tok), F32),
                jax.ShapeDtypeStruct((1, state, width), F32),
            ),
            in_specs=[vspec] * 4,
            out_specs=(vspec,) * 4,
            scratch_shapes=[
                vm((state, width), F32),
                vm((seq_bits, state, width), F32),
                vm((state, width), F32),
                vm((state, width), F32),
                vm((bits, half, width), F32),
                vm((half, width), F32),
                vm((bits, half, width), F32),
                vm((bits, half, width), F32),
                vm((bits, half, width), F32),
                vm((bits, state, width), F32),
                vm((slots, half, width), F32),
                vm((bits, half, width), F32),
                vm((half, width), F32),
                vm((half, width), F32),
                vm((state, width), F32),
                vm((seq_bits, state, width), BF16),
                vm((state, width), BF16),
                vm((seq_bits, tok, width), BF16),
                vm((tok, width), F32),
                vm((tok, tok), F32),
                vm((tok, state), F32),
                vm((head_parts, tok // head_parts, state), F32),
                vm((2, tok, tok), F32),
                pltpu.SemaphoreType.DMA((len(send.table),)),
                pltpu.SemaphoreType.DMA((len(recv.table),)),
            ],
            compiler_params=pltpu.CompilerParams(
                collective_id=0, has_side_effects=True, vmem_limit_bytes=56 * 1024 * 1024),
        )(qk_proj, values, out_grad, level_weights)

    return jax.shard_map(
        body, mesh=mesh,
        in_specs=(P("seq", None), P("seq", "head"), P("seq", "head"), P("head", None, "seq")),
        out_specs=(P(("seq", "head"), None), P("seq", "head"), P("head", None, "seq"), P("seq", None, "head")),
        check_vma=False)
```

```python
import functools

import jax
import jax.numpy as jnp
from jax import lax
from jax.experimental import pallas as pl
from jax.experimental.pallas import tpu as pltpu
from jax.sharding import PartitionSpec as P

MESH = pl.DeviceIdType.MESH
CHUNKS = 8
F32 = jnp.float32
BF16 = jnp.bfloat16


def dot(a, b, ca, cb):
    return lax.dot_general(a, b, (((ca,), (cb,)), ((), ())), preferred_element_type=F32)


class Ids:
    def __init__(self):
        self.table = {}

    def __call__(self, *key):
        return self.table.setdefault(key, len(self.table))


def sem_ids(heads, chip_bits):
    ids = Ids()
    for r in range(CHUNKS):
        ids("xa", r), ids("xb", r), ids("rd", r)
        for k in range(chip_bits):
            ids("xd", k, r), ids("ru", k, r), ids("up", k, r), ids("dn", k, r), ids("dc", k, r)
    ids("xc")
    for i in range(1, heads):
        ids("rs", i)
    return ids


def kernel(chips, head_parts, seq_bits, qk_ref, v_ref, g_ref, lw_ref, qg_ref, vg_ref, lam_ref, car_ref,
           own, gst, xup, xd0, xd, bz, gz, acc, dsum, lst, dcon, drec, bh, bo, bst, low, blow, sc, vloc, at, qp, rs,
           lev_ref, ssem, rsem):
    tok, state = qk_ref.shape
    width = v_ref.shape[1]
    nheads, levels = lw_ref.shape[0], lw_ref.shape[1]
    hdim = width // nheads
    tok_bits = tok.bit_length() - 1
    chip_bits = seq_bits - 1
    half = state // 2
    rows = half // CHUNKS
    sid = sem_ids(head_parts, chip_bits)

    seq, hd = lax.axis_index("seq"), lax.axis_index("head")
    core, z = seq % 2, seq // 2
    partner = seq + 1 - 2 * core

    def bit(k):
        return (z // (1 << k)) % 2

    def at_chip(chip):
        return {"seq": chip * 2 + core}

    mines = [pl.ds(pl.multiple_of(core * half + r * rows, rows), rows) for r in range(CHUNKS)]
    others = [pl.ds(pl.multiple_of((1 - core) * half + r * rows, rows), rows) for r in range(CHUNKS)]
    mine, other = mines.__getitem__, others.__getitem__

    def part(r):
        return pl.ds(r * rows, rows)

    started = []

    def send(cond, src, dst, key, device):
        pltpu.make_async_remote_copy(
            src_ref=src, dst_ref=dst, send_sem=ssem.at[sid(*key)], recv_sem=rsem.at[sid(*key)],
            device_id=device, device_id_type=MESH).start()
        started.append((cond, key))

    def sent(skey):
        like = xd0 if skey[0] == "xc" else rs.at[skey[1]] if skey[0] == "rs" else bz.at[part(0)]
        pltpu.make_async_remote_copy(
            src_ref=like, dst_ref=like, send_sem=ssem.at[sid(*skey)], recv_sem=rsem.at[0],
            device_id={"seq": partner}, device_id_type=MESH).wait_send()

    def arrive(ref, key):
        pltpu.make_async_remote_copy(
            src_ref=ref, dst_ref=ref, send_sem=ssem.at[0], recv_sem=rsem.at[sid(*key)],
            device_id={"seq": partner}, device_id_type=MESH).wait_recv()

    barrier = pltpu.get_barrier_semaphore()
    pl.semaphore_signal(barrier, inc=1, device_id={"seq": partner}, device_id_type=MESH)
    for i in range(1, chips):
        pl.semaphore_signal(barrier, inc=1, device_id=at_chip((z + i) % chips), device_id_type=MESH)
    for i in range(1, head_parts):
        pl.semaphore_signal(barrier, inc=1, device_id={"head": (hd + i) % head_parts}, device_id_type=MESH)

    qk = qk_ref[...]
    own[...] = dot(qk, v_ref[...], 0, 0)
    pl.semaphore_wait(barrier, 1 + (chips - 1) + (head_parts - 1))
    for r in range(CHUNKS):
        send(None, own.at[other(r)], xup.at[other(r)], ("xa", r), {"seq": partner})

    spread = (lax.broadcasted_iota(jnp.int32, (nheads, width), 1) // hdim
              == lax.broadcasted_iota(jnp.int32, (nheads, width), 0)).astype(F32).astype(BF16)

    def grad_state(b):
        weight = lw_ref[:, tok_bits + 1 + b, :]
        first = weight.astype(BF16)
        rest = weight - first.astype(F32)
        second = rest.astype(BF16)
        third = (rest - second.astype(F32)).astype(BF16)
        scale = dot(first, spread, 0, 0) + (dot(second, spread, 0, 0) + dot(third, spread, 0, 0))
        scaled = (scale * g_ref[...].astype(F32)).astype(BF16)
        sc[b] = scaled
        gst[b] = dot(qk, scaled, 0, 0)

    for k in range(chip_bits - 1, -1, -1):
        grad_state(k + 1)
        for r in range(CHUNKS):
            send(None, gst.at[k + 1, other(r)], xd.at[k, part(r)], ("xd", k, r), {"seq": partner})

    lower = bit(0) == 0
    for r in range(CHUNKS):
        arrive(xup.at[mine(r)], ("xa", r))
        bz[part(r)] = own[mine(r)] + xup[mine(r)]
        if chip_bits:
            @pl.when(lower)
            def _():
                send(lower, bz.at[part(r)], lst.at[0, mine(r)], ("up", 0, r), at_chip(z + 1))

    for k in range(chip_bits - 1, -1, -1):
        size = 1 << k
        top = (bit(k) == 1) & (z % size == size - 1)
        for r in range(CHUNKS):
            arrive(xd.at[k, part(r)], ("xd", k, r))
            gz[k, part(r)] = gst[k + 1, mine(r)] + xd[k, part(r)]

            @pl.when(top)
            def _():
                if k == 0:
                    send(top, gz.at[0, part(r)], drec.at[0, part(r)], ("dn", 0, r), at_chip(z - 1))
                else:
                    send(top, gz.at[k, part(r)], dcon.at[k, part(r)], ("dc", k, r), at_chip(z - 1))

    cond_low = core == 0
    cond_high = core == 1

    @pl.when(cond_low)
    def _():
        for r in range(CHUNKS):
            send(cond_low, own.at[mine(r)], xup.at[mine(r)], ("xb", r), {"seq": partner})

    grad_state(0)

    @pl.when(cond_high)
    def _():
        send(cond_high, gst.at[0], xd0, ("xc",), {"seq": partner})

    key_at = lax.broadcasted_iota(jnp.int32, (tok, tok), 0)
    query_at = lax.broadcasted_iota(jnp.int32, (tok, tok), 1)
    crossed = key_at ^ query_at
    found = jnp.zeros((tok, tok), jnp.int32)
    for exponent in range(tok_bits):
        found = found + jnp.where(crossed >= (1 << exponent), 1, 0)
    lev_ref[0] = jnp.where(key_at <= query_at, found, -1).astype(F32)
    lev_ref[1] = dot(qk, qk, 1, 1)
    at[...] = jnp.zeros_like(at)
    lam_ref[:, tok_bits + 1 + seq_bits:, :] = jnp.zeros((nheads, levels - tok_bits - 1 - seq_bits, tok), F32)

    def head_group(head, cols, count):
        vals, grads = v_ref[:, cols], g_ref[:, cols]
        lane_head = lax.broadcasted_iota(jnp.int32, vals.shape, 1) // hdim
        score_parts, grad_parts = [], []
        total = at[...]
        for j in range(count):
            vals_j = vals if count == 1 else jnp.where(lane_head == j, vals, jnp.zeros_like(vals))
            grads_j = grads if count == 1 else jnp.where(lane_head == j, grads, jnp.zeros_like(grads))
            pair = dot(vals_j, grads, 1, 1)
            lev, score = lev_ref[0], lev_ref[1]
            weights = lw_ref[head + j]
            product = score * pair
            local = jnp.zeros((tok, tok), F32)
            sums = []
            for level in range(tok_bits + 1):
                here = lev == float(level)
                local = jnp.where(here, weights[level:level + 1, :], local)
                sums.append(jnp.sum(jnp.where(here, product, 0.0), axis=0, keepdims=True))
            lam_ref[head + j, 0:tok_bits + 1, :] = jnp.concatenate(sums, axis=0)
            score_parts.append((local * score).astype(BF16))
            grad_parts.append(grads_j)
            total = total + (local * pair).astype(BF16).astype(F32)
        at[...] = total
        out = dot(score_parts[0], grad_parts[0], 1, 0)
        for j in range(1, count):
            out = out + dot(score_parts[j], grad_parts[j], 1, 0)
        vloc[:, cols] = out

    per = max(1, 128 // hdim)
    groups = nheads // per

    def run_groups(start, stop):
        @pl.loop(start, stop)
        def _(p):
            head_group(p * per, pl.ds(pl.multiple_of(p * per * hdim, per * hdim), per * hdim), per)

    def up_step(k, r):
        size = 1 << k
        cond = bit(k) == 1
        if k:
            onward = cond & (z % size != size - 1)

            @pl.when(onward)
            def _():
                arrive(lst.at[k, mine(r)], ("up", k, r))
                send(onward, lst.at[k, mine(r)], lst.at[k, mine(r)], ("up", k, r), at_chip(z + 1))
                send(onward, lst.at[k, mine(r)], lst.at[k, mine(r)], ("ru", k, r), {"seq": partner})

            last = cond & (z % size == size - 1)
        else:
            last = cond

        @pl.when(last)
        def _():
            arrive(lst.at[k, mine(r)], ("up", k, r))
            send(last, lst.at[k, mine(r)], lst.at[k, mine(r)], ("ru", k, r), {"seq": partner})

        kk = k + 1
        if kk < chip_bits:
            cond_s = (z % (1 << kk) == (1 << kk) - 1) & (bit(kk) == 0)

            @pl.when(cond_s)
            def _():
                value = bz[part(r)]
                for j in range(kk):
                    value = value + lst[j, mine(r)]
                acc[kk, part(r)] = value
                send(cond_s, acc.at[kk, part(r)], lst.at[kk, mine(r)], ("up", kk, r), at_chip(z + 1))

    def sum_step(k, r):
        size = 1 << k

        def joined():
            arrive(dcon.at[k, part(r)], ("dc", k, r))
            dsum[k, part(r)] = gz[k, part(r)] + dcon[k, part(r)]

        bottom = (bit(k) == 1) & (z % size == 0)

        @pl.when(bottom)
        def _():
            joined()
            send(bottom, dsum.at[k, part(r)], drec.at[k, part(r)], ("dn", k, r), at_chip(z - 1))

        if k > 1:
            middle = (bit(k) == 1) & (z % size != 0) & (z % size != size - 1)

            @pl.when(middle)
            def _():
                joined()
                send(middle, dsum.at[k, part(r)], dcon.at[k, part(r)], ("dc", k, r), at_chip(z - 1))

    has_back = z != chips - 1

    def down_step(k, r):
        size = 1 << k
        first = k == chip_bits - 1
        cond = bit(k) == 0

        @pl.when(cond)
        def _():
            arrive(drec.at[k, part(r)], ("dn", k, r))

        if k:
            onward = cond & (z % size != 0)

            @pl.when(onward)
            def _():
                send(onward, drec.at[k, part(r)], drec.at[k, part(r)], ("dn", k, r), at_chip(z - 1))

        @pl.when(cond)
        def _():
            bh[part(r)] = drec[k, part(r)] if first else bh[part(r)] + drec[k, part(r)]

        if first:
            @pl.when(jnp.logical_not(cond))
            def _():
                bh[part(r)] = jnp.zeros((rows, width), F32)

        if k == 0:
            @pl.when(has_back)
            def _():
                send(has_back, bh.at[part(r)], bo.at[part(r)], ("rd", r), {"seq": partner})

    def cross(b):
        state_low = low[b]
        readout = dot(qk, state_low, 1, 0)
        product = readout * g_ref[...].astype(F32)
        high = product.astype(BF16)
        rest = (product - high.astype(F32)).astype(BF16)
        lam_ref[:, tok_bits + 1 + b, :] = dot(spread, high, 1, 1) + dot(spread, rest, 1, 1)
        part_b = dot(sc[b], state_low, 1, 1)
        if b == 0:
            qp[...] = part_b
        else:
            qp[...] = qp[...] + part_b

    def level_zero():
        @pl.when(core == 1)
        def _():
            for r in range(CHUNKS):
                arrive(xup.at[other(r)], ("xb", r))
            low[0] = xup[...].astype(BF16)
            car_ref[0] = xup[...]

        @pl.when(core == 0)
        def _():
            low[0] = jnp.zeros((state, width), BF16)
            car_ref[0] = jnp.zeros((state, width), F32)

        cross(0)

    def level_up(k):
        cond = bit(k) == 1

        @pl.when(cond)
        def _():
            for r in range(CHUNKS):
                arrive(lst.at[k, other(r)], ("ru", k, r))
            low[k + 1] = lst[k].astype(BF16)
            car_ref[0] = car_ref[0] + lst[k]

        @pl.when(jnp.logical_not(cond))
        def _():
            low[k + 1] = jnp.zeros((state, width), BF16)

        cross(k + 1)

    steps = []
    for k in range(chip_bits - 1):
        for r in range(CHUNKS):
            steps.append(lambda r=r, k=k: up_step(k, r))
            steps.append(lambda r=r, k=chip_bits - 1 - k: sum_step(k, r))
        if k == 0:
            steps.append(level_zero)
        else:
            steps.append(lambda k=k: level_up(k - 1))
    for r in range(CHUNKS):
        steps.append(lambda r=r: up_step(chip_bits - 1, r))
        steps.append(lambda r=r: down_step(chip_bits - 1, r))
    if chip_bits > 1:
        steps.append(lambda: level_up(chip_bits - 2))
    for k in range(chip_bits - 2, -1, -1):
        steps += [(lambda r=r, k=k: down_step(k, r)) for r in range(CHUNKS)]
    slots = min(10, max(1, groups))
    done = 0
    for n, step in enumerate(steps):
        upto = groups * min(slots, n * slots // len(steps) + 1) // slots
        if upto > done:
            run_groups(done, upto)
            done = upto
        step()
    if done < groups:
        run_groups(done, groups)
    for h in range(groups * per, nheads):
        head_group(h, pl.ds(h * hdim, hdim), 1)

    high = at[...].astype(BF16)
    rest = (at[...] - high.astype(F32)).astype(BF16)
    qp[...] = qp[...] + (dot(high, qk, 1, 0) + dot(high, qk, 0, 0)) + (dot(rest, qk, 1, 0) + dot(rest, qk, 0, 0))

    level_up(chip_bits - 1)

    @pl.when(has_back)
    def _():
        for r in range(CHUNKS):
            arrive(bo.at[part(r)], ("rd", r))
            bst[mine(r)] = bh[part(r)]
            bst[other(r)] = bo[part(r)]

    @pl.when(jnp.logical_not(has_back))
    def _():
        bst[...] = jnp.zeros((state, width), F32)

    @pl.when(core == 0)
    def _():
        arrive(xd0, ("xc",))
        blow[...] = (bst[...] + xd0[...]).astype(BF16)

    @pl.when(core == 1)
    def _():
        blow[...] = bst[...].astype(BF16)

    back = blow[...]
    qp[...] = qp[...] + dot(v_ref[...], back, 1, 1)
    share = tok // head_parts
    for i in range(1, head_parts):
        to = (hd + i) % head_parts
        send(None, qp.at[pl.ds(pl.multiple_of(to * share, share), share)], rs.at[i], ("rs", i), {"head": to})
    vg_ref[...] = (vloc[...] + dot(qk, back, 1, 0)).astype(BF16)
    total = qp[pl.ds(pl.multiple_of(hd * share, share), share)]
    for i in range(1, head_parts):
        arrive(rs.at[i], ("rs", i))
        total = total + rs[i]
    qg_ref[...] = total

    for cond, skey in started:
        if cond is None:
            sent(skey)
        else:
            @pl.when(cond)
            def _():
                sent(skey)


def write_out(*refs):
    sources, targets, sems = refs[:4], refs[4:8], refs[8]
    copies = [pltpu.make_async_copy(source, target, sems.at[i]) for i, (source, target) in enumerate(zip(sources, targets))]
    for copy in copies:
        copy.start()
    for copy in copies:
        copy.wait()


def solution(mesh):
    chips = mesh.shape["seq"] // 2
    head_parts = mesh.shape["head"]
    seq_bits = mesh.shape["seq"].bit_length() - 1
    chip_bits = seq_bits - 1

    def body(qk_proj, values, out_grad, level_weights):
        tok, state = qk_proj.shape
        width = values.shape[1]
        nheads, levels = level_weights.shape[:2]
        half = state // 2
        copies = len(sem_ids(head_parts, chip_bits).table)
        bits = max(1, chip_bits)
        vm = pltpu.VMEM
        vspec = pl.BlockSpec(memory_space=pltpu.VMEM)
        shapes = (
            ((tok // head_parts, state), F32),
            ((tok, width), BF16),
            ((nheads, levels, tok), F32),
            ((1, state, width), F32),
        )
        results = pl.pallas_call(
            functools.partial(kernel, chips, head_parts, seq_bits),
            out_shape=tuple(pltpu.VMEM(shape, kind) for shape, kind in shapes),
            in_specs=[vspec] * 4,
            out_specs=(vspec,) * 4,
            scratch_shapes=[
                vm((state, width), F32),
                vm((seq_bits, state, width), F32),
                vm((state, width), F32),
                vm((state, width), F32),
                vm((bits, half, width), F32),
                vm((half, width), F32),
                vm((bits, half, width), F32),
                vm((bits, half, width), F32),
                vm((bits, half, width), F32),
                vm((bits, state, width), F32),
                vm((bits, half, width), F32),
                vm((bits, half, width), F32),
                vm((half, width), F32),
                vm((half, width), F32),
                vm((state, width), F32),
                vm((seq_bits, state, width), BF16),
                vm((state, width), BF16),
                vm((seq_bits, tok, width), BF16),
                vm((tok, width), F32),
                vm((tok, tok), F32),
                vm((tok, state), F32),
                vm((head_parts, tok // head_parts, state), F32),
                vm((2, tok, tok), F32),
                pltpu.SemaphoreType.DMA((copies,)),
                pltpu.SemaphoreType.DMA((copies,)),
            ],
            compiler_params=pltpu.CompilerParams(
                collective_id=0, has_side_effects=True, vmem_limit_bytes=56 * 1024 * 1024),
        )(qk_proj, values, out_grad, level_weights)
        return pl.pallas_call(
            write_out,
            out_shape=tuple(jax.ShapeDtypeStruct(shape, kind) for shape, kind in shapes),
            in_specs=[vspec] * 4,
            out_specs=(pl.BlockSpec(memory_space=pl.ANY),) * 4,
            scratch_shapes=[pltpu.SemaphoreType.DMA((4,))],
        )(*(pltpu.with_memory_space_constraint(x, pltpu.VMEM) for x in results))

    return jax.shard_map(
        body, mesh=mesh,
        in_specs=(P("seq", None), P("seq", "head"), P("seq", "head"), P("head", None, "seq")),
        out_specs=(P(("seq", "head"), None), P("seq", "head"), P("head", None, "seq"), P("seq", None, "head")),
        check_vma=False)
```

```python
import functools

import jax
import jax.numpy as jnp
from jax import lax
from jax.experimental import pallas as pl
from jax.experimental.pallas import tpu as pltpu
from jax.sharding import PartitionSpec as P

MESH = pl.DeviceIdType.MESH
CHUNKS = 4
F32 = jnp.float32
BF16 = jnp.bfloat16


def dot(a, b, ca, cb):
    return lax.dot_general(a, b, (((ca,), (cb,)), ((), ())), preferred_element_type=F32)


class Ids:
    def __init__(self):
        self.table = {}

    def __call__(self, *key):
        return self.table.setdefault(key, len(self.table))


def sem_ids(heads, chip_bits):
    ids = Ids()
    for r in range(CHUNKS):
        ids("xa", r), ids("xb", r), ids("rd", r)
        for k in range(chip_bits):
            ids("xd", k, r), ids("ru", k, r), ids("up", k, r), ids("dn", k, r), ids("dc", k, r)
    ids("xc")
    for i in range(1, heads):
        ids("rs", i)
    return ids


def kernel(chips, head_parts, seq_bits, qk_in, v_in, g_in, lw_in, qg_ref, vg_ref, lam_ref, car_ref,
           own, gst, xup, xd0, xd, bz, gz, acc, dsum, lst, dcon, drec, bh, bo, bst, low, blow, sc, vloc, at, qp, rs,
           lev_ref, qk_ref, v_ref, g_ref, lw_ref, isem, ssem, rsem):
    loads = [pltpu.make_async_copy(source, target, isem.at[i]) for i, (source, target) in
             enumerate(((qk_in, qk_ref), (v_in, v_ref), (g_in, g_ref), (lw_in, lw_ref)))]
    for load in loads:
        load.start()
    tok, state = qk_ref.shape
    width = v_ref.shape[1]
    nheads, levels = lw_ref.shape[0], lw_ref.shape[1]
    hdim = width // nheads
    tok_bits = tok.bit_length() - 1
    chip_bits = seq_bits - 1
    half = state // 2
    rows = half // CHUNKS
    sid = sem_ids(head_parts, chip_bits)

    seq, hd = lax.axis_index("seq"), lax.axis_index("head")
    core, z = seq % 2, seq // 2
    partner = seq + 1 - 2 * core

    def bit(k):
        return (z // (1 << k)) % 2

    def at_chip(chip):
        return {"seq": chip * 2 + core}

    mines = [pl.ds(pl.multiple_of(core * half + r * rows, rows), rows) for r in range(CHUNKS)]
    others = [pl.ds(pl.multiple_of((1 - core) * half + r * rows, rows), rows) for r in range(CHUNKS)]
    mine, other = mines.__getitem__, others.__getitem__

    def part(r):
        return pl.ds(r * rows, rows)

    started = []

    def send(cond, src, dst, key, device):
        pltpu.make_async_remote_copy(
            src_ref=src, dst_ref=dst, send_sem=ssem.at[sid(*key)], recv_sem=rsem.at[sid(*key)],
            device_id=device, device_id_type=MESH).start()
        started.append((cond, key))

    def sent(skey):
        like = xd0 if skey[0] == "xc" else rs.at[skey[1]] if skey[0] == "rs" else bz.at[part(0)]
        pltpu.make_async_remote_copy(
            src_ref=like, dst_ref=like, send_sem=ssem.at[sid(*skey)], recv_sem=rsem.at[0],
            device_id={"seq": partner}, device_id_type=MESH).wait_send()

    def arrive(ref, key):
        pltpu.make_async_remote_copy(
            src_ref=ref, dst_ref=ref, send_sem=ssem.at[0], recv_sem=rsem.at[sid(*key)],
            device_id={"seq": partner}, device_id_type=MESH).wait_recv()

    barrier = pltpu.get_barrier_semaphore()
    pl.semaphore_signal(barrier, inc=1, device_id={"seq": partner}, device_id_type=MESH)
    for i in range(1, chips):
        pl.semaphore_signal(barrier, inc=1, device_id=at_chip((z + i) % chips), device_id_type=MESH)
    for i in range(1, head_parts):
        pl.semaphore_signal(barrier, inc=1, device_id={"head": (hd + i) % head_parts}, device_id_type=MESH)

    loads[0].wait()
    loads[1].wait()
    qk = qk_ref[...]
    own[...] = dot(qk, v_ref[...], 0, 0)
    pl.semaphore_wait(barrier, 1 + (chips - 1) + (head_parts - 1))
    for r in range(CHUNKS):
        send(None, own.at[other(r)], xup.at[other(r)], ("xa", r), {"seq": partner})

    loads[2].wait()
    loads[3].wait()
    spread = (lax.broadcasted_iota(jnp.int32, (nheads, width), 1) // hdim
              == lax.broadcasted_iota(jnp.int32, (nheads, width), 0)).astype(F32).astype(BF16)

    def grad_state(b):
        weight = lw_ref[:, tok_bits + 1 + b, :]
        first = weight.astype(BF16)
        rest = weight - first.astype(F32)
        second = rest.astype(BF16)
        third = (rest - second.astype(F32)).astype(BF16)
        scale = dot(first, spread, 0, 0) + (dot(second, spread, 0, 0) + dot(third, spread, 0, 0))
        scaled = (scale * g_ref[...].astype(F32)).astype(BF16)
        sc[b] = scaled
        gst[b] = dot(qk, scaled, 0, 0)

    for k in range(chip_bits - 1, -1, -1):
        grad_state(k + 1)
        for r in range(CHUNKS):
            send(None, gst.at[k + 1, other(r)], xd.at[k, part(r)], ("xd", k, r), {"seq": partner})

    lower = bit(0) == 0
    for r in range(CHUNKS):
        arrive(xup.at[mine(r)], ("xa", r))
        bz[part(r)] = own[mine(r)] + xup[mine(r)]
        if chip_bits:
            @pl.when(lower)
            def _():
                send(lower, bz.at[part(r)], lst.at[0, mine(r)], ("up", 0, r), at_chip(z + 1))

    for k in range(chip_bits - 1, -1, -1):
        size = 1 << k
        top = (bit(k) == 1) & (z % size == size - 1)
        for r in range(CHUNKS):
            arrive(xd.at[k, part(r)], ("xd", k, r))
            gz[k, part(r)] = gst[k + 1, mine(r)] + xd[k, part(r)]

            @pl.when(top)
            def _():
                if k == 0:
                    send(top, gz.at[0, part(r)], drec.at[0, part(r)], ("dn", 0, r), at_chip(z - 1))
                else:
                    send(top, gz.at[k, part(r)], dcon.at[k, part(r)], ("dc", k, r), at_chip(z - 1))

    cond_low = core == 0
    cond_high = core == 1

    @pl.when(cond_low)
    def _():
        for r in range(CHUNKS):
            send(cond_low, own.at[mine(r)], xup.at[mine(r)], ("xb", r), {"seq": partner})

    grad_state(0)

    @pl.when(cond_high)
    def _():
        send(cond_high, gst.at[0], xd0, ("xc",), {"seq": partner})

    key_at = lax.broadcasted_iota(jnp.int32, (tok, tok), 0)
    query_at = lax.broadcasted_iota(jnp.int32, (tok, tok), 1)
    crossed = key_at ^ query_at
    found = jnp.zeros((tok, tok), jnp.int32)
    for exponent in range(tok_bits):
        found = found + jnp.where(crossed >= (1 << exponent), 1, 0)
    lev_ref[0] = jnp.where(key_at <= query_at, found, -1).astype(F32)
    lev_ref[1] = dot(qk, qk, 1, 1)
    at[...] = jnp.zeros_like(at)
    lam_ref[:, tok_bits + 1 + seq_bits:, :] = jnp.zeros((nheads, levels - tok_bits - 1 - seq_bits, tok), F32)

    def head_group(head, cols, count):
        vals, grads = v_ref[:, cols], g_ref[:, cols]
        lane_head = lax.broadcasted_iota(jnp.int32, vals.shape, 1) // hdim
        score_parts, grad_parts = [], []
        total = at[...]
        for j in range(count):
            vals_j = vals if count == 1 else jnp.where(lane_head == j, vals, jnp.zeros_like(vals))
            grads_j = grads if count == 1 else jnp.where(lane_head == j, grads, jnp.zeros_like(grads))
            pair = dot(vals_j, grads, 1, 1)
            lev, score = lev_ref[0], lev_ref[1]
            weights = lw_ref[head + j]
            product = score * pair
            local = jnp.zeros((tok, tok), F32)
            sums = []
            for level in range(tok_bits + 1):
                here = lev == float(level)
                local = jnp.where(here, weights[level:level + 1, :], local)
                sums.append(jnp.sum(jnp.where(here, product, 0.0), axis=0, keepdims=True))
            lam_ref[head + j, 0:tok_bits + 1, :] = jnp.concatenate(sums, axis=0)
            score_parts.append((local * score).astype(BF16))
            grad_parts.append(grads_j)
            total = total + (local * pair).astype(BF16).astype(F32)
        at[...] = total
        out = dot(score_parts[0], grad_parts[0], 1, 0)
        for j in range(1, count):
            out = out + dot(score_parts[j], grad_parts[j], 1, 0)
        vloc[:, cols] = out

    per = max(1, 128 // hdim)
    groups = nheads // per

    def run_groups(start, stop):
        @pl.loop(start, stop)
        def _(p):
            head_group(p * per, pl.ds(pl.multiple_of(p * per * hdim, per * hdim), per * hdim), per)

    def up_step(k, r):
        size = 1 << k
        cond = bit(k) == 1
        if k:
            onward = cond & (z % size != size - 1)

            @pl.when(onward)
            def _():
                arrive(lst.at[k, mine(r)], ("up", k, r))
                send(onward, lst.at[k, mine(r)], lst.at[k, mine(r)], ("up", k, r), at_chip(z + 1))
                send(onward, lst.at[k, mine(r)], lst.at[k, mine(r)], ("ru", k, r), {"seq": partner})

            last = cond & (z % size == size - 1)
        else:
            last = cond

        @pl.when(last)
        def _():
            arrive(lst.at[k, mine(r)], ("up", k, r))
            send(last, lst.at[k, mine(r)], lst.at[k, mine(r)], ("ru", k, r), {"seq": partner})

        kk = k + 1
        if kk < chip_bits:
            cond_s = (z % (1 << kk) == (1 << kk) - 1) & (bit(kk) == 0)

            @pl.when(cond_s)
            def _():
                value = bz[part(r)]
                for j in range(kk):
                    value = value + lst[j, mine(r)]
                acc[kk, part(r)] = value
                send(cond_s, acc.at[kk, part(r)], lst.at[kk, mine(r)], ("up", kk, r), at_chip(z + 1))

    def sum_step(k, r):
        size = 1 << k

        def joined():
            arrive(dcon.at[k, part(r)], ("dc", k, r))
            dsum[k, part(r)] = gz[k, part(r)] + dcon[k, part(r)]

        bottom = (bit(k) == 1) & (z % size == 0)

        @pl.when(bottom)
        def _():
            joined()
            send(bottom, dsum.at[k, part(r)], drec.at[k, part(r)], ("dn", k, r), at_chip(z - 1))

        if k > 1:
            middle = (bit(k) == 1) & (z % size != 0) & (z % size != size - 1)

            @pl.when(middle)
            def _():
                joined()
                send(middle, dsum.at[k, part(r)], dcon.at[k, part(r)], ("dc", k, r), at_chip(z - 1))

    has_back = z != chips - 1

    def down_step(k, r):
        size = 1 << k
        first = k == chip_bits - 1
        cond = bit(k) == 0

        @pl.when(cond)
        def _():
            arrive(drec.at[k, part(r)], ("dn", k, r))

        if k:
            onward = cond & (z % size != 0)

            @pl.when(onward)
            def _():
                send(onward, drec.at[k, part(r)], drec.at[k, part(r)], ("dn", k, r), at_chip(z - 1))

        @pl.when(cond)
        def _():
            bh[part(r)] = drec[k, part(r)] if first else bh[part(r)] + drec[k, part(r)]

        if first:
            @pl.when(jnp.logical_not(cond))
            def _():
                bh[part(r)] = jnp.zeros((rows, width), F32)

        if k == 0:
            @pl.when(has_back)
            def _():
                send(has_back, bh.at[part(r)], bo.at[part(r)], ("rd", r), {"seq": partner})

    def query(b):
        part_b = dot(sc[b], low[b], 1, 1)
        qp[...] = part_b if b == 0 else qp[...] + part_b

    def level_sums(b):
        product = dot(qk, low[b], 1, 0) * g_ref[...].astype(F32)
        high = product.astype(BF16)
        rest = (product - high.astype(F32)).astype(BF16)
        lam_ref[:, tok_bits + 1 + b, :] = dot(spread, high, 1, 1) + dot(spread, rest, 1, 1)

    def level_zero():
        @pl.when(core == 1)
        def _():
            for r in range(CHUNKS):
                arrive(xup.at[other(r)], ("xb", r))
            low[0] = xup[...].astype(BF16)
            car_ref[0] = xup[...]

        @pl.when(core == 0)
        def _():
            low[0] = jnp.zeros((state, width), BF16)
            car_ref[0] = jnp.zeros((state, width), F32)

        query(0)
        level_sums(0)

    def level_arrive(k):
        cond = bit(k) == 1

        @pl.when(cond)
        def _():
            for r in range(CHUNKS):
                arrive(lst.at[k, other(r)], ("ru", k, r))
            low[k + 1] = lst[k].astype(BF16)

        @pl.when(jnp.logical_not(cond))
        def _():
            low[k + 1] = jnp.zeros((state, width), BF16)

        query(k + 1)

    def level_finish(k):
        @pl.when(bit(k) == 1)
        def _():
            car_ref[0] = car_ref[0] + lst[k]

        level_sums(k + 1)

    def level_up(k):
        level_arrive(k)
        level_finish(k)

    steps = []
    final = chip_bits - 1
    early = []
    for k in range(final):
        for r in range(CHUNKS):
            early.append((lambda r=r, k=k: up_step(k, r), lambda r=r, k=final - k: sum_step(k, r)))
        early.append((level_zero,) if k == 0 else (lambda k=k: level_up(k - 1),))
    late = [(lambda r=r: up_step(final, r), lambda r=r: down_step(final, r)) for r in range(CHUNKS)]
    if not early:
        early = [(level_zero,)]
    lead = len(early) - CHUNKS + 1 if final == 1 else len(early)
    steps += [one for pair in early[:lead] for one in pair]
    for pair, after in zip(late, early[lead:] + [()] * CHUNKS):
        steps += list(pair) + list(after)
    for after in early[lead:][CHUNKS:]:
        steps += list(after)
    if final > 0:
        steps.append(lambda: level_up(final - 1))
    for k in range(final - 1, -1, -1):
        steps += [(lambda r=r, k=k: down_step(k, r)) for r in range(CHUNKS)]
    slots = min(10, max(1, groups))
    done = 0
    for n, step in enumerate(steps):
        upto = groups * min(slots, n * slots // len(steps) + 1) // slots
        if upto > done:
            run_groups(done, upto)
            done = upto
        step()
    if done < groups:
        run_groups(done, groups)
    for h in range(groups * per, nheads):
        head_group(h, pl.ds(h * hdim, hdim), 1)

    high = at[...].astype(BF16)
    rest = (at[...] - high.astype(F32)).astype(BF16)
    qp[...] = qp[...] + (dot(high, qk, 1, 0) + dot(high, qk, 0, 0)) + (dot(rest, qk, 1, 0) + dot(rest, qk, 0, 0))

    level_arrive(final)

    @pl.when(has_back)
    def _():
        for r in range(CHUNKS):
            arrive(bo.at[part(r)], ("rd", r))
            bst[mine(r)] = bh[part(r)]
            bst[other(r)] = bo[part(r)]

    @pl.when(jnp.logical_not(has_back))
    def _():
        bst[...] = jnp.zeros((state, width), F32)

    @pl.when(core == 0)
    def _():
        arrive(xd0, ("xc",))
        blow[...] = (bst[...] + xd0[...]).astype(BF16)

    @pl.when(core == 1)
    def _():
        blow[...] = bst[...].astype(BF16)

    back = blow[...]
    qp[...] = qp[...] + dot(v_ref[...], back, 1, 1)
    share = tok // head_parts
    for i in range(1, head_parts):
        to = (hd + i) % head_parts
        send(None, qp.at[pl.ds(pl.multiple_of(to * share, share), share)], rs.at[i], ("rs", i), {"head": to})
    level_finish(final)
    vg_ref[...] = (vloc[...] + dot(qk, back, 1, 0)).astype(BF16)
    total = qp[pl.ds(pl.multiple_of(hd * share, share), share)]
    for i in range(1, head_parts):
        arrive(rs.at[i], ("rs", i))
        total = total + rs[i]
    qg_ref[...] = total

    for cond, skey in started:
        if cond is None:
            sent(skey)
        else:
            @pl.when(cond)
            def _():
                sent(skey)


def write_out(*refs):
    sources, targets, sems = refs[:4], refs[4:8], refs[8]
    copies = [pltpu.make_async_copy(source, target, sems.at[i]) for i, (source, target) in enumerate(zip(sources, targets))]
    for copy in copies:
        copy.start()
    for copy in copies:
        copy.wait()


def solution(mesh):
    chips = mesh.shape["seq"] // 2
    head_parts = mesh.shape["head"]
    seq_bits = mesh.shape["seq"].bit_length() - 1
    chip_bits = seq_bits - 1

    def body(qk_proj, values, out_grad, level_weights):
        tok, state = qk_proj.shape
        width = values.shape[1]
        nheads, levels = level_weights.shape[:2]
        half = state // 2
        copies = len(sem_ids(head_parts, chip_bits).table)
        bits = max(1, chip_bits)
        vm = pltpu.VMEM
        vspec = pl.BlockSpec(memory_space=pltpu.VMEM)
        shapes = (
            ((tok // head_parts, state), F32),
            ((tok, width), BF16),
            ((nheads, levels, tok), F32),
            ((1, state, width), F32),
        )
        results = pl.pallas_call(
            functools.partial(kernel, chips, head_parts, seq_bits),
            out_shape=tuple(pltpu.VMEM(shape, kind) for shape, kind in shapes),
            in_specs=[pl.BlockSpec(memory_space=pl.ANY)] * 4,
            out_specs=(vspec,) * 4,
            scratch_shapes=[
                vm((state, width), F32),
                vm((seq_bits, state, width), F32),
                vm((state, width), F32),
                vm((state, width), F32),
                vm((bits, half, width), F32),
                vm((half, width), F32),
                vm((bits, half, width), F32),
                vm((bits, half, width), F32),
                vm((bits, half, width), F32),
                vm((bits, state, width), F32),
                vm((bits, half, width), F32),
                vm((bits, half, width), F32),
                vm((half, width), F32),
                vm((half, width), F32),
                vm((state, width), F32),
                vm((seq_bits, state, width), BF16),
                vm((state, width), BF16),
                vm((seq_bits, tok, width), BF16),
                vm((tok, width), F32),
                vm((tok, tok), F32),
                vm((tok, state), F32),
                vm((head_parts, tok // head_parts, state), F32),
                vm((2, tok, tok), F32),
                vm((tok, state), BF16),
                vm((tok, width), BF16),
                vm((tok, width), BF16),
                vm((nheads, levels, tok), F32),
                pltpu.SemaphoreType.DMA((4,)),
                pltpu.SemaphoreType.DMA((copies,)),
                pltpu.SemaphoreType.DMA((copies,)),
            ],
            compiler_params=pltpu.CompilerParams(
                collective_id=0, has_side_effects=True, vmem_limit_bytes=56 * 1024 * 1024),
        )(qk_proj, values, out_grad, level_weights)
        return pl.pallas_call(
            write_out,
            out_shape=tuple(jax.ShapeDtypeStruct(shape, kind) for shape, kind in shapes),
            in_specs=[vspec] * 4,
            out_specs=(pl.BlockSpec(memory_space=pl.ANY),) * 4,
            scratch_shapes=[pltpu.SemaphoreType.DMA((4,))],
        )(*(pltpu.with_memory_space_constraint(x, pltpu.VMEM) for x in results))

    return jax.shard_map(
        body, mesh=mesh,
        in_specs=(P("seq", None), P("seq", "head"), P("seq", "head"), P("head", None, "seq")),
        out_specs=(P(("seq", "head"), None), P("seq", "head"), P("head", None, "seq"), P("seq", None, "head")),
        check_vma=False)
```

```python
import functools

import jax
import jax.numpy as jnp
from jax import lax
from jax.experimental import pallas as pl
from jax.experimental.pallas import tpu as pltpu
from jax.sharding import PartitionSpec as P

MESH = pl.DeviceIdType.MESH
CHUNKS = 4
F32 = jnp.float32
BF16 = jnp.bfloat16


def dot(a, b, ca, cb):
    return lax.dot_general(a, b, (((ca,), (cb,)), ((), ())), preferred_element_type=F32)


class Ids:
    def __init__(self):
        self.table = {}

    def __call__(self, *key):
        return self.table.setdefault(key, len(self.table))


def sem_ids(heads, chip_bits):
    ids = Ids()
    for r in range(CHUNKS):
        ids("xa", r), ids("xb", r), ids("rd", r)
        for k in range(chip_bits):
            ids("xd", k, r), ids("ru", k, r), ids("up", k, r), ids("dn", k, r), ids("dc", k, r)
    ids("xc")
    for i in range(1, heads):
        ids("rs", i)
    return ids


def kernel(chips, head_parts, seq_bits, qk_in, v_in, g_in, lw_in, qg_ref, vg_ref, lam_ref, car_ref,
           own, gst, xup, xd0, xd, bz, gz, acc, dsum, lst, dcon, drec, bh, bo, bst, low, blow, sc, vloc, at, qp, rs,
           lev_ref, qk_ref, v_ref, g_ref, lw_ref, isem, ssem, rsem):
    loads = [pltpu.make_async_copy(source, target, isem.at[i]) for i, (source, target) in
             enumerate(((qk_in, qk_ref), (v_in, v_ref), (g_in, g_ref), (lw_in, lw_ref)))]
    for load in loads:
        load.start()
    tok, state = qk_ref.shape
    width = v_ref.shape[1]
    nheads, levels = lw_ref.shape[0], lw_ref.shape[1]
    hdim = width // nheads
    tok_bits = tok.bit_length() - 1
    chip_bits = seq_bits - 1
    half = state // 2
    rows = half // CHUNKS
    sid = sem_ids(head_parts, chip_bits)

    seq, hd = lax.axis_index("seq"), lax.axis_index("head")
    core, z = seq % 2, seq // 2
    partner = seq + 1 - 2 * core

    def bit(k):
        return (z // (1 << k)) % 2

    def at_chip(chip):
        return {"seq": chip * 2 + core}

    mines = [pl.ds(pl.multiple_of(core * half + r * rows, rows), rows) for r in range(CHUNKS)]
    others = [pl.ds(pl.multiple_of((1 - core) * half + r * rows, rows), rows) for r in range(CHUNKS)]
    mine, other = mines.__getitem__, others.__getitem__

    def part(r):
        return pl.ds(r * rows, rows)

    started = []

    def send(cond, src, dst, key, device):
        pltpu.make_async_remote_copy(
            src_ref=src, dst_ref=dst, send_sem=ssem.at[sid(*key)], recv_sem=rsem.at[sid(*key)],
            device_id=device, device_id_type=MESH).start()
        started.append((cond, key))

    def sent(skey):
        like = xd0 if skey[0] == "xc" else rs.at[skey[1]] if skey[0] == "rs" else bz.at[part(0)]
        pltpu.make_async_remote_copy(
            src_ref=like, dst_ref=like, send_sem=ssem.at[sid(*skey)], recv_sem=rsem.at[0],
            device_id={"seq": partner}, device_id_type=MESH).wait_send()

    def arrive(ref, key):
        pltpu.make_async_remote_copy(
            src_ref=ref, dst_ref=ref, send_sem=ssem.at[0], recv_sem=rsem.at[sid(*key)],
            device_id={"seq": partner}, device_id_type=MESH).wait_recv()

    barrier = pltpu.get_barrier_semaphore()
    pl.semaphore_signal(barrier, inc=1, device_id={"seq": partner}, device_id_type=MESH)
    for i in range(1, chips):
        pl.semaphore_signal(barrier, inc=1, device_id=at_chip((z + i) % chips), device_id_type=MESH)
    for i in range(1, head_parts):
        pl.semaphore_signal(barrier, inc=1, device_id={"head": (hd + i) % head_parts}, device_id_type=MESH)

    loads[0].wait()
    loads[1].wait()
    qk = qk_ref[...]
    own[...] = dot(qk, v_ref[...], 0, 0)
    pl.semaphore_wait(barrier, 1 + (chips - 1) + (head_parts - 1))
    for r in range(CHUNKS):
        send(None, own.at[other(r)], xup.at[other(r)], ("xa", r), {"seq": partner})

    loads[2].wait()
    loads[3].wait()
    spread = (lax.broadcasted_iota(jnp.int32, (nheads, width), 1) // hdim
              == lax.broadcasted_iota(jnp.int32, (nheads, width), 0)).astype(F32).astype(BF16)

    def grad_state(b):
        weight = lw_ref[:, tok_bits + 1 + b, :]
        first = weight.astype(BF16)
        rest = weight - first.astype(F32)
        second = rest.astype(BF16)
        third = (rest - second.astype(F32)).astype(BF16)
        scale = dot(first, spread, 0, 0) + (dot(second, spread, 0, 0) + dot(third, spread, 0, 0))
        scaled = (scale * g_ref[...].astype(F32)).astype(BF16)
        sc[b] = scaled
        gst[b] = dot(qk, scaled, 0, 0)

    for k in range(chip_bits - 1, -1, -1):
        grad_state(k + 1)
        for r in range(CHUNKS):
            send(None, gst.at[k + 1, other(r)], xd.at[k, part(r)], ("xd", k, r), {"seq": partner})

    lower = bit(0) == 0
    for r in range(CHUNKS):
        arrive(xup.at[mine(r)], ("xa", r))
        bz[part(r)] = own[mine(r)] + xup[mine(r)]
        if chip_bits:
            @pl.when(lower)
            def _():
                send(lower, bz.at[part(r)], lst.at[0, mine(r)], ("up", 0, r), at_chip(z + 1))

    for k in range(chip_bits - 1, -1, -1):
        size = 1 << k
        top = (bit(k) == 1) & (z % size == size - 1)
        for r in range(CHUNKS):
            arrive(xd.at[k, part(r)], ("xd", k, r))
            gz[k, part(r)] = gst[k + 1, mine(r)] + xd[k, part(r)]

            @pl.when(top)
            def _():
                if k == 0:
                    send(top, gz.at[0, part(r)], drec.at[0, part(r)], ("dn", 0, r), at_chip(z - 1))
                else:
                    send(top, gz.at[k, part(r)], dcon.at[k, part(r)], ("dc", k, r), at_chip(z - 1))

    cond_low = core == 0
    cond_high = core == 1

    @pl.when(cond_low)
    def _():
        for r in range(CHUNKS):
            send(cond_low, own.at[mine(r)], xup.at[mine(r)], ("xb", r), {"seq": partner})

    grad_state(0)

    @pl.when(cond_high)
    def _():
        send(cond_high, gst.at[0], xd0, ("xc",), {"seq": partner})

    key_at = lax.broadcasted_iota(jnp.int32, (tok, tok), 0)
    query_at = lax.broadcasted_iota(jnp.int32, (tok, tok), 1)
    crossed = key_at ^ query_at
    found = jnp.zeros((tok, tok), jnp.int32)
    for exponent in range(tok_bits):
        found = found + jnp.where(crossed >= (1 << exponent), 1, 0)
    lev_ref[0] = jnp.where(key_at <= query_at, found, -1).astype(F32)
    lev_ref[1] = dot(qk, qk, 1, 1)
    at[...] = jnp.zeros_like(at)
    lam_ref[:, tok_bits + 1 + seq_bits:, :] = jnp.zeros((nheads, levels - tok_bits - 1 - seq_bits, tok), F32)

    def head_group(head, cols, count):
        vals, grads = v_ref[:, cols], g_ref[:, cols]
        lane_head = lax.broadcasted_iota(jnp.int32, vals.shape, 1) // hdim
        score_parts, grad_parts = [], []
        total = at[...]
        for j in range(count):
            vals_j = vals if count == 1 else jnp.where(lane_head == j, vals, jnp.zeros_like(vals))
            grads_j = grads if count == 1 else jnp.where(lane_head == j, grads, jnp.zeros_like(grads))
            pair = dot(vals_j, grads, 1, 1)
            lev, score = lev_ref[0], lev_ref[1]
            weights = lw_ref[head + j]
            product = score * pair
            local = jnp.zeros((tok, tok), F32)
            sums = []
            for level in range(tok_bits + 1):
                here = lev == float(level)
                local = jnp.where(here, weights[level:level + 1, :], local)
                sums.append(jnp.sum(jnp.where(here, product, 0.0), axis=0, keepdims=True))
            lam_ref[head + j, 0:tok_bits + 1, :] = jnp.concatenate(sums, axis=0)
            score_parts.append((local * score).astype(BF16))
            grad_parts.append(grads_j)
            total = total + (local * pair).astype(BF16).astype(F32)
        at[...] = total
        out = dot(score_parts[0], grad_parts[0], 1, 0)
        for j in range(1, count):
            out = out + dot(score_parts[j], grad_parts[j], 1, 0)
        vloc[:, cols] = out

    per = max(1, 128 // hdim)
    groups = nheads // per

    def run_groups(start, stop):
        @pl.loop(start, stop)
        def _(p):
            head_group(p * per, pl.ds(pl.multiple_of(p * per * hdim, per * hdim), per * hdim), per)

    def up_step(k, r):
        size = 1 << k
        cond = bit(k) == 1
        if k:
            onward = cond & (z % size != size - 1)

            @pl.when(onward)
            def _():
                arrive(lst.at[k, mine(r)], ("up", k, r))
                send(onward, lst.at[k, mine(r)], lst.at[k, mine(r)], ("up", k, r), at_chip(z + 1))
                send(onward, lst.at[k, mine(r)], lst.at[k, mine(r)], ("ru", k, r), {"seq": partner})

            last = cond & (z % size == size - 1)
        else:
            last = cond

        @pl.when(last)
        def _():
            arrive(lst.at[k, mine(r)], ("up", k, r))
            send(last, lst.at[k, mine(r)], lst.at[k, mine(r)], ("ru", k, r), {"seq": partner})

        kk = k + 1
        if kk < chip_bits:
            cond_s = (z % (1 << kk) == (1 << kk) - 1) & (bit(kk) == 0)

            @pl.when(cond_s)
            def _():
                value = bz[part(r)]
                for j in range(kk):
                    value = value + lst[j, mine(r)]
                acc[kk, part(r)] = value
                send(cond_s, acc.at[kk, part(r)], lst.at[kk, mine(r)], ("up", kk, r), at_chip(z + 1))

    def sum_step(k, r):
        size = 1 << k

        def joined():
            arrive(dcon.at[k, part(r)], ("dc", k, r))
            dsum[k, part(r)] = gz[k, part(r)] + dcon[k, part(r)]

        bottom = (bit(k) == 1) & (z % size == 0)

        @pl.when(bottom)
        def _():
            joined()
            send(bottom, dsum.at[k, part(r)], drec.at[k, part(r)], ("dn", k, r), at_chip(z - 1))

        if k > 1:
            middle = (bit(k) == 1) & (z % size != 0) & (z % size != size - 1)

            @pl.when(middle)
            def _():
                joined()
                send(middle, dsum.at[k, part(r)], dcon.at[k, part(r)], ("dc", k, r), at_chip(z - 1))

    has_back = z != chips - 1

    def down_step(k, r):
        size = 1 << k
        first = k == chip_bits - 1
        cond = bit(k) == 0

        @pl.when(cond)
        def _():
            arrive(drec.at[k, part(r)], ("dn", k, r))

        if k:
            onward = cond & (z % size != 0)

            @pl.when(onward)
            def _():
                send(onward, drec.at[k, part(r)], drec.at[k, part(r)], ("dn", k, r), at_chip(z - 1))

        @pl.when(cond)
        def _():
            bh[part(r)] = drec[k, part(r)] if first else bh[part(r)] + drec[k, part(r)]

        if first:
            @pl.when(jnp.logical_not(cond))
            def _():
                bh[part(r)] = jnp.zeros((rows, width), F32)

        if k == 0:
            @pl.when(has_back)
            def _():
                send(has_back, bh.at[part(r)], bo.at[part(r)], ("rd", r), {"seq": partner})

    def query(b):
        part_b = dot(sc[b], low[b], 1, 1)
        qp[...] = part_b if b == 0 else qp[...] + part_b

    def level_sums(b):
        product = dot(qk, low[b], 1, 0) * g_ref[...].astype(F32)
        high = product.astype(BF16)
        rest = (product - high.astype(F32)).astype(BF16)
        lam_ref[:, tok_bits + 1 + b, :] = dot(spread, high, 1, 1) + dot(spread, rest, 1, 1)

    def level_zero():
        @pl.when(core == 1)
        def _():
            for r in range(CHUNKS):
                arrive(xup.at[other(r)], ("xb", r))
            low[0] = xup[...].astype(BF16)
            car_ref[0] = xup[...]

        @pl.when(core == 0)
        def _():
            low[0] = jnp.zeros((state, width), BF16)
            car_ref[0] = jnp.zeros((state, width), F32)

        query(0)
        level_sums(0)

    def level_arrive(k):
        cond = bit(k) == 1

        @pl.when(cond)
        def _():
            for r in range(CHUNKS):
                arrive(lst.at[k, other(r)], ("ru", k, r))
            low[k + 1] = lst[k].astype(BF16)

        @pl.when(jnp.logical_not(cond))
        def _():
            low[k + 1] = jnp.zeros((state, width), BF16)

        query(k + 1)

    def level_finish(k):
        @pl.when(bit(k) == 1)
        def _():
            car_ref[0] = car_ref[0] + lst[k]

        level_sums(k + 1)

    def level_up(k):
        level_arrive(k)
        level_finish(k)

    steps = []
    final = chip_bits - 1
    early = []
    for k in range(final):
        for r in range(CHUNKS):
            early.append((lambda r=r, k=k: up_step(k, r), lambda r=r, k=final - k: sum_step(k, r)))
        early.append((level_zero,) if k == 0 else (lambda k=k: level_up(k - 1),))
    late = [(lambda r=r: up_step(final, r), lambda r=r: down_step(final, r)) for r in range(CHUNKS)]
    if not early:
        early = [(level_zero,)]
    lead = len(early) - CHUNKS + 2 if final == 1 else len(early)
    steps += [one for pair in early[:lead] for one in pair]
    for pair, after in zip(late, early[lead:] + [()] * CHUNKS):
        steps += list(pair) + list(after)
    for after in early[lead:][CHUNKS:]:
        steps += list(after)
    if final > 0:
        steps.append(lambda: level_up(final - 1))
    for k in range(final - 1, -1, -1):
        steps += [(lambda r=r, k=k: down_step(k, r)) for r in range(CHUNKS)]
    slots = min(10, max(1, groups))
    done = 0
    for n, step in enumerate(steps):
        upto = groups * min(slots, n * slots // len(steps) + 1) // slots
        if upto > done:
            run_groups(done, upto)
            done = upto
        step()
    if done < groups:
        run_groups(done, groups)
    for h in range(groups * per, nheads):
        head_group(h, pl.ds(h * hdim, hdim), 1)

    high = at[...].astype(BF16)
    rest = (at[...] - high.astype(F32)).astype(BF16)
    qp[...] = qp[...] + (dot(high, qk, 1, 0) + dot(high, qk, 0, 0)) + (dot(rest, qk, 1, 0) + dot(rest, qk, 0, 0))

    level_arrive(final)

    @pl.when(has_back)
    def _():
        for r in range(CHUNKS):
            arrive(bo.at[part(r)], ("rd", r))
            bst[mine(r)] = bh[part(r)]
            bst[other(r)] = bo[part(r)]

    @pl.when(jnp.logical_not(has_back))
    def _():
        bst[...] = jnp.zeros((state, width), F32)

    @pl.when(core == 0)
    def _():
        arrive(xd0, ("xc",))
        blow[...] = (bst[...] + xd0[...]).astype(BF16)

    @pl.when(core == 1)
    def _():
        blow[...] = bst[...].astype(BF16)

    back = blow[...]
    qp[...] = qp[...] + dot(v_ref[...], back, 1, 1)
    share = tok // head_parts
    for i in range(1, head_parts):
        to = (hd + i) % head_parts
        send(None, qp.at[pl.ds(pl.multiple_of(to * share, share), share)], rs.at[i], ("rs", i), {"head": to})
    level_finish(final)
    vg_ref[...] = (vloc[...] + dot(qk, back, 1, 0)).astype(BF16)
    total = qp[pl.ds(pl.multiple_of(hd * share, share), share)]
    for i in range(1, head_parts):
        arrive(rs.at[i], ("rs", i))
        total = total + rs[i]
    qg_ref[...] = total

    for cond, skey in started:
        if cond is None:
            sent(skey)
        else:
            @pl.when(cond)
            def _():
                sent(skey)


def write_out(*refs):
    sources, targets, sems = refs[:4], refs[4:8], refs[8]
    copies = [pltpu.make_async_copy(source, target, sems.at[i]) for i, (source, target) in enumerate(zip(sources, targets))]
    for copy in copies:
        copy.start()
    for copy in copies:
        copy.wait()


def solution(mesh):
    chips = mesh.shape["seq"] // 2
    head_parts = mesh.shape["head"]
    seq_bits = mesh.shape["seq"].bit_length() - 1
    chip_bits = seq_bits - 1

    def body(qk_proj, values, out_grad, level_weights):
        tok, state = qk_proj.shape
        width = values.shape[1]
        nheads, levels = level_weights.shape[:2]
        half = state // 2
        copies = len(sem_ids(head_parts, chip_bits).table)
        bits = max(1, chip_bits)
        vm = pltpu.VMEM
        vspec = pl.BlockSpec(memory_space=pltpu.VMEM)
        shapes = (
            ((tok // head_parts, state), F32),
            ((tok, width), BF16),
            ((nheads, levels, tok), F32),
            ((1, state, width), F32),
        )
        results = pl.pallas_call(
            functools.partial(kernel, chips, head_parts, seq_bits),
            out_shape=tuple(pltpu.VMEM(shape, kind) for shape, kind in shapes),
            in_specs=[pl.BlockSpec(memory_space=pl.ANY)] * 4,
            out_specs=(vspec,) * 4,
            scratch_shapes=[
                vm((state, width), F32),
                vm((seq_bits, state, width), F32),
                vm((state, width), F32),
                vm((state, width), F32),
                vm((bits, half, width), F32),
                vm((half, width), F32),
                vm((bits, half, width), F32),
                vm((bits, half, width), F32),
                vm((bits, half, width), F32),
                vm((bits, state, width), F32),
                vm((bits, half, width), F32),
                vm((bits, half, width), F32),
                vm((half, width), F32),
                vm((half, width), F32),
                vm((state, width), F32),
                vm((seq_bits, state, width), BF16),
                vm((state, width), BF16),
                vm((seq_bits, tok, width), BF16),
                vm((tok, width), F32),
                vm((tok, tok), F32),
                vm((tok, state), F32),
                vm((head_parts, tok // head_parts, state), F32),
                vm((2, tok, tok), F32),
                vm((tok, state), BF16),
                vm((tok, width), BF16),
                vm((tok, width), BF16),
                vm((nheads, levels, tok), F32),
                pltpu.SemaphoreType.DMA((4,)),
                pltpu.SemaphoreType.DMA((copies,)),
                pltpu.SemaphoreType.DMA((copies,)),
            ],
            compiler_params=pltpu.CompilerParams(
                collective_id=0, has_side_effects=True, vmem_limit_bytes=56 * 1024 * 1024),
        )(qk_proj, values, out_grad, level_weights)
        return pl.pallas_call(
            write_out,
            out_shape=tuple(jax.ShapeDtypeStruct(shape, kind) for shape, kind in shapes),
            in_specs=[vspec] * 4,
            out_specs=(pl.BlockSpec(memory_space=pl.ANY),) * 4,
            scratch_shapes=[pltpu.SemaphoreType.DMA((4,))],
        )(*(pltpu.with_memory_space_constraint(x, pltpu.VMEM) for x in results))

    return jax.shard_map(
        body, mesh=mesh,
        in_specs=(P("seq", None), P("seq", "head"), P("seq", "head"), P("head", None, "seq")),
        out_specs=(P(("seq", "head"), None), P("seq", "head"), P("head", None, "seq"), P("seq", None, "head")),
        check_vma=False)
```
